32 devices in a mesh: dp: 8 (over y, x, core), tensor: 4 (over z).
Axes of the slice: x: 2, y: 2, z: 4, core: 2. Of those that a mesh axis runs over, the one named last changes fastest.
Arguments:
- tokens: bfloat16 [1024, 8192], P('dp'), may hold values from -6 to 6
- target: bfloat16 [1024, 8192], P('dp'), may hold values from -6 to 6
- weight_in: bfloat16 [8192, 16384], P('dp', 'tensor'), may hold values from -0.125 to 0.125
- weight_out: bfloat16 [16384, 8192], P('tensor', 'dp'), may hold values from -0.09375 to 0.09375
- pattern: int32 [64, 128], replicated, may hold values from 0 to 1, as said below
Outputs:
- output: bfloat16 [1024, 8192], P('dp', 'tensor')
- hidden_target: bfloat16 [1024, 16384], P('dp', 'tensor')
The draws below stay inside these ranges and needn't reach their ends.
Inputs may be any that keep to these rules, and one draw needn't show every extreme that they name: `pattern`: every entry is 0 or 1. A tile is the 8 row blocks of one index of dp with the 32 hidden blocks of one index of tensor; no tile holds more than 64 ones, and in every draw all tiles of one index of tensor hold exactly 64.
All inputs are finite; a program needn't handle non-finite values.
Results may differ from the reference program's by a relative error of at most 0.013.
Values may be sent and summed in bfloat16 or wider, within the bound.
A program may use at most 128 MiB of HBM per device.

```python
import jax
import jax.numpy as jnp
from jax import lax

D = 8192
H = 16384
BLK = 128
TOK_DEV = 128
TOKENS = 1024
RB = 64
HB = 128
RB_DEV = 8
HB_DEV = 32
TILE = 256
CAP = 64
N_DP = 8
N_TENSOR = 4


def draw_pattern(key, part):
    fewest = max(1, CAP // 4)
    most_other = max(fewest, CAP * 3 // 4)
    busiest = jax.random.randint(jax.random.fold_in(key, 11), (), 0, N_TENSOR)
    counts = jax.random.randint(jax.random.fold_in(key, 12), (N_DP, N_TENSOR), fewest, most_other + 1)
    counts = jnp.where(jnp.arange(N_TENSOR)[None, :] == busiest, CAP, counts)
    tile_keys = jax.random.split(jax.random.fold_in(key, 13), N_DP * N_TENSOR)

    def shuffle(single):
        return jax.random.permutation(single, TILE)
    orders = jax.vmap(shuffle)(tile_keys)
    present = (orders < counts.reshape(N_DP * N_TENSOR, 1)).astype(jnp.int32)
    blocks_mask = present.reshape(N_DP, N_TENSOR, RB_DEV, HB_DEV).transpose(0, 2, 1, 3)
    return blocks_mask.reshape(RB, HB)


def level_of(key, extent, cuts, smallest, largest):
    gain = 1.0
    for axis_at, parts in cuts:
        steps = jax.random.uniform(jax.random.fold_in(jax.random.fold_in(key, 6), axis_at), (parts,), jnp.float32, smallest / len(cuts), largest / len(cuts))
        gain = gain * jnp.repeat(jnp.exp(steps), extent[axis_at] // parts).reshape((-1,) + (1,) * (len(extent) - 1 - axis_at))
    return gain


def noise(rng, shape, deviation, limit, shards=(), dtype=jnp.bfloat16):
    array = jax.random.normal(rng, shape, jnp.float32) * deviation
    if len(shards) > 0:
        array = level_of(rng, shape, shards, -0.22, 0.18) * array
    return jnp.clip(array, min=-limit, max=limit).astype(dtype)


def setup_inputs(seed: int = 0) -> dict:
    seeds = jax.random.split(jax.random.key(seed), 6)
    return {
        "tokens": noise(seeds[0], (TOKENS, D), 1.0, 6.0, ((0, 8),)),
        "target": noise(seeds[1], (TOKENS, D), 1.0, 6.0, ((0, 8),)),
        "weight_in": noise(seeds[2], (D, H), (D // 4) ** -0.5, 0.125, ((0, 8), (1, 4))),
        "weight_out": noise(seeds[3], (H, D), (H // 4) ** -0.5, 0.09375, ((0, 4), (1, 8))),
        "pattern": draw_pattern(jax.random.fold_in(seeds[5], 71), 0),
    }


def reference(tokens, target, weight_in, weight_out, pattern):
    block_mask = jnp.repeat(jnp.repeat(pattern, BLK, axis=0), BLK, axis=1).astype(jnp.bfloat16)
    kept_in = weight_in * block_mask
    kept_out = weight_out * block_mask.T
    kept_back = kept_out.T
    group_width = H // N_TENSOR

    def one_block(block_pair):
        token_rows, goal_rows = block_pair
        hidden = jnp.dot(token_rows, kept_in, preferred_element_type=jnp.float32)
        active = jnp.tanh(hidden).astype(jnp.bfloat16)
        summed = jnp.zeros((token_rows.shape[0], D), jnp.float32)
        for group_index in range(N_TENSOR):
            first = group_index * group_width
            partial_value = jnp.dot(active[:, first:first + group_width], kept_out[first:first + group_width], preferred_element_type=jnp.float32).astype(jnp.bfloat16)
            partial_value = lax.optimization_barrier(partial_value)
            summed = summed + partial_value.astype(jnp.float32)
        output = summed.astype(jnp.bfloat16)
        stacked = jnp.concatenate([output, goal_rows], axis=0)
        image = jnp.dot(stacked, kept_back, preferred_element_type=jnp.float32)
        feedback = jnp.tanh(image)
        row_count = token_rows.shape[0]
        hidden_target = (active.astype(jnp.float32) + feedback[row_count:] - feedback[:row_count]).astype(jnp.bfloat16)
        return output, hidden_target

    outputs, targets = lax.map(one_block, (tokens.reshape(N_DP, TOK_DEV, D), target.reshape(N_DP, TOK_DEV, D)))
    return outputs.reshape(TOKENS, D), targets.reshape(TOKENS, H)
```

```python
import jax
import jax.numpy as jnp
from jax import lax
from jax.experimental import pallas as pl
from jax.experimental.pallas import tpu as pltpu
from jax.sharding import PartitionSpec as P

BLK = 128
UNROLL = 8
PIECES = 4
VMEM_CAP = 60 * 1024 * 1024


def tile_slots(strip, peer_count, capacity):
    rows, across = strip.shape
    flat = strip.reshape(peer_count, rows // peer_count * across)
    position = jnp.cumsum(flat, axis=1) - 1
    base = jnp.arange(peer_count, dtype=jnp.int32)[:, None] * capacity
    return (position + base).reshape(rows, across), position


def pair_lists(strip, slot, axis, slots):
    rows, across = strip.shape
    kept = strip.shape[1 - axis]
    pairs = -(-((slots + kept) // 2) // UNROLL) * UNROLL
    rank = jnp.cumsum(strip, axis=axis) - 1
    runs = (jnp.sum(strip, axis=axis) + 1) // 2
    start = 2 * (jnp.cumsum(runs) - runs)
    place = rank + jnp.expand_dims(start, axis)
    row = lax.broadcasted_iota(jnp.int32, strip.shape, 0)
    column = lax.broadcasted_iota(jnp.int32, strip.shape, 1)
    code = ((slot + 1) * rows + row) * across + column
    place = jnp.where(strip == 1, place, -1).reshape(1, -1)
    hit = place == jnp.arange(2 * pairs, dtype=jnp.int32)[:, None]
    found = jnp.sum(jnp.where(hit, code.reshape(1, -1), 0), axis=1)
    valid = (found > 0).astype(jnp.int32)
    source = jnp.maximum(found // (rows * across) - 1, 0)
    row_of = (found // across) % rows
    column_of = found % across
    over, along = (row_of, column_of) if axis == 0 else (column_of, row_of)
    return source, over, along[::2], valid


def pack_kernel(rows_ref, cols_ref, in_ref, out_ref, packed_in, packed_out, sems):
    count = packed_in.shape[0]

    def start(s, carry):
        r = pl.multiple_of(rows_ref[s] * BLK, BLK)
        j = pl.multiple_of(cols_ref[s] * BLK, BLK)
        pltpu.make_async_copy(
            in_ref.at[pl.ds(r, BLK), pl.ds(j, BLK)], packed_in.at[s], sems.at[0]
        ).start()
        pltpu.make_async_copy(
            out_ref.at[pl.ds(j, BLK), pl.ds(r, BLK)], packed_out.at[s], sems.at[1]
        ).start()
        return carry

    lax.fori_loop(0, count, start, 0)
    pltpu.make_async_copy(packed_in, packed_in, sems.at[0]).wait()
    pltpu.make_async_copy(packed_out, packed_out, sems.at[1]).wait()


def pack(rows, cols, weight_in, weight_out, capacity):
    shape = jax.ShapeDtypeStruct((capacity, BLK, BLK), jnp.bfloat16)
    return pl.pallas_call(
        pack_kernel,
        grid_spec=pltpu.PrefetchScalarGridSpec(
            num_scalar_prefetch=2,
            grid=(1,),
            in_specs=[pl.BlockSpec(memory_space=pl.ANY)] * 2,
            out_specs=[pl.BlockSpec((capacity, BLK, BLK), lambda i, *_: (0, 0, 0))] * 2,
            scratch_shapes=[pltpu.SemaphoreType.DMA((2,))],
        ),
        out_shape=(shape, shape),
        name="pack",
    )(rows, cols, weight_in, weight_out)


def gather_kernel(in_ref, out_ref, all_in, all_out, send, recv, local):
    me = lax.axis_index("dp")
    core, x, y = me % 2, (me // 2) % 2, me // 4

    def index(c, x_at, y_at):
        return (y_at * 2 + x_at) * 2 + c

    beside = index(core, 1 - x, y)
    above = index(core, x, 1 - y)
    across = index(core, 1 - x, 1 - y)
    partner = index(1 - core, x, y)
    barrier = pltpu.get_barrier_semaphore()
    for other in (beside, above, partner):
        pl.semaphore_signal(
            barrier, inc=1, device_id={"dp": other}, device_id_type=pl.DeviceIdType.MESH
        )
    pl.semaphore_wait(barrier, 3)

    count = in_ref.shape[0]
    pieces = PIECES if count % PIECES == 0 else 1
    size = count // pieces
    steps = range(2 * pieces)

    def own(k):
        return (in_ref, out_ref)[k // pieces].at[pl.ds((k % pieces) * size, size)]

    def held(owner, k):
        ref = (all_in, all_out)[k // pieces]
        return ref.at[pl.ds(owner * count + (k % pieces) * size, size)]

    started = []

    def move(path, k, source, owner, to):
        copy = pltpu.make_async_remote_copy(
            src_ref=source,
            dst_ref=held(owner, k),
            send_sem=send.at[path, k],
            recv_sem=recv.at[path, k],
            device_id={"dp": to},
            device_id_type=pl.DeviceIdType.MESH,
        )
        copy.start()
        started.append(copy)

    def arrive(path, k, owner, to):
        pltpu.make_async_remote_copy(
            src_ref=held(owner, k),
            dst_ref=held(owner, k),
            send_sem=send.at[path, k],
            recv_sem=recv.at[path, k],
            device_id={"dp": to},
            device_id_type=pl.DeviceIdType.MESH,
        ).wait_recv()

    for k in steps:
        move(0, k, own(k), me, beside)
        move(1, k, own(k), me, above)
        move(2, k, own(k), me, partner)
    copies = [
        pltpu.make_async_copy(own(k), held(me, k), local.at[k]) for k in steps
    ]
    for copy in copies:
        copy.start()
    for k in steps:
        arrive(0, k, beside, beside)
        if k % 2 == 0:
            move(3, k, held(beside, k), beside, above)
        move(5, k, held(beside, k), beside, partner)
        arrive(1, k, above, above)
        if k % 2 == 1:
            move(4, k, held(above, k), above, beside)
        move(6, k, held(above, k), above, partner)
    for k in steps:
        if k % 2 == 0:
            arrive(3, k, across, above)
        else:
            arrive(4, k, across, beside)
        move(7, k, held(across, k), across, partner)
    for k in steps:
        arrive(2, k, partner, partner)
        arrive(5, k, index(1 - core, 1 - x, y), partner)
        arrive(6, k, index(1 - core, x, 1 - y), partner)
        arrive(7, k, index(1 - core, 1 - x, 1 - y), partner)
    for copy in started:
        copy.wait_send()
    for copy in copies:
        copy.wait()


def gather(packed_in, packed_out, peers):
    if peers != 8:
        return (
            lax.all_gather(packed_in, "dp", axis=0, tiled=True),
            lax.all_gather(packed_out, "dp", axis=0, tiled=True),
        )
    count = packed_in.shape[0]
    shape = jax.ShapeDtypeStruct((peers * count, BLK, BLK), jnp.bfloat16)
    pieces = PIECES if count % PIECES == 0 else 1
    return pl.pallas_call(
        gather_kernel,
        out_shape=(shape, shape),
        in_specs=[pl.BlockSpec(memory_space=pltpu.VMEM)] * 2,
        out_specs=[pl.BlockSpec(memory_space=pl.ANY)] * 2,
        scratch_shapes=[
            pltpu.SemaphoreType.DMA((8, 2 * pieces)),
            pltpu.SemaphoreType.DMA((8, 2 * pieces)),
            pltpu.SemaphoreType.DMA((2 * pieces,)),
        ],
        compiler_params=pltpu.CompilerParams(collective_id=0, has_side_effects=True),
        name="gather",
    )(packed_in, packed_out)


def sweep(lists, lhs_ref, w_ref, acc, pairs, transposed):
    source, over, along, valid = lists
    acc[...] = jnp.zeros_like(acc)

    def one(p):
        parts, weights = [], []
        for k in (2 * p, 2 * p + 1):
            off = pl.multiple_of(over[k] * BLK, BLK)
            part = lhs_ref[:, pl.ds(off, BLK)]
            parts.append(jnp.where(valid[k] == 1, part, jnp.zeros_like(part)))
            weights.append(w_ref[source[k]])
        lhs = jnp.concatenate(parts, axis=1)
        if transposed:
            rhs = jnp.concatenate(weights, axis=1)
            dims = (((1,), (1,)), ((), ()))
        else:
            rhs = jnp.concatenate(weights, axis=0)
            dims = (((1,), (0,)), ((), ()))
        return along[p], lax.dot_general(lhs, rhs, dims, preferred_element_type=jnp.float32)

    def body(i, carry):
        results = [one(i * UNROLL + u) for u in range(UNROLL)]
        for place, value in results:
            acc[place] += value
        return carry

    lax.fori_loop(0, pairs // UNROLL, body, 0)


def spread(acc, out_ref, finish):
    def body(j, carry):
        at = pl.ds(pl.multiple_of(j * BLK, BLK), BLK)
        out_ref[:, at] = finish(acc[j], at)
        return carry

    lax.fori_loop(0, acc.shape[0], body, 0)


def hidden_kernel(source, over, along, valid, lhs, w, active, acc):
    sweep((source, over, along, valid), lhs, w, acc, along.shape[0], False)
    spread(acc, active, lambda a, at: jnp.tanh(a).astype(jnp.bfloat16))


def emit_kernel(source, over, along, valid, lhs, w, partial, acc):
    sweep((source, over, along, valid), lhs, w, acc, along.shape[0], False)
    spread(acc, partial, lambda a, at: a.astype(jnp.bfloat16))


def goal_kernel(source, over, along, valid, lhs, w, active, goal, acc):
    sweep((source, over, along, valid), lhs, w, acc, along.shape[0], True)
    spread(acc, goal, lambda a, at: active[:, at].astype(jnp.float32) + jnp.tanh(a))


def correct_kernel(source, over, along, valid, lhs, w, goal, result, acc):
    sweep((source, over, along, valid), lhs, w, acc, along.shape[0], True)
    spread(acc, result, lambda a, at: (goal[:, at] - jnp.tanh(a)).astype(jnp.bfloat16))


def run(kernel, name, lists, arrays, blocks, dtype):
    tok = arrays[0].shape[0]
    pairs = lists[2].shape[0]
    return pl.pallas_call(
        kernel,
        grid_spec=pltpu.PrefetchScalarGridSpec(
            num_scalar_prefetch=4,
            grid=(1,),
            in_specs=[
                pl.BlockSpec(a.shape, lambda i, *_, n=a.ndim: (0,) * n, pipeline_mode=pl.Buffered(1))
                for a in arrays
            ],
            out_specs=pl.BlockSpec((tok, blocks * BLK), lambda i, *_: (0, 0)),
            scratch_shapes=[pltpu.VMEM((blocks, tok, BLK), jnp.float32)],
        ),
        out_shape=jax.ShapeDtypeStruct((tok, blocks * BLK), dtype),
        compiler_params=pltpu.CompilerParams(vmem_limit_bytes=VMEM_CAP),
        cost_estimate=pl.CostEstimate(
            flops=pairs * 4 * tok * BLK * BLK * 4,
            bytes_accessed=sum(a.size * a.dtype.itemsize for a in arrays),
            transcendentals=0,
        ),
        name=name,
    )(*lists, *arrays)


def shards(tokens, target, weight_in, weight_out, pattern):
    peers = lax.axis_size("dp")
    data_rank = lax.axis_index("dp")
    tensor_rank = lax.axis_index("tensor")
    down = weight_in.shape[0] // BLK
    across = weight_in.shape[1] // BLK
    capacity = max(2, down * across // 4)
    slots = peers * capacity
    all_rows = tokens.shape[1] // BLK
    strip = lax.dynamic_slice_in_dim(pattern, tensor_rank * across, across, 1)
    slot, position = tile_slots(strip, peers, capacity)

    own_mask = lax.dynamic_index_in_dim(
        strip.reshape(peers, down * across), data_rank, 0, keepdims=False
    )
    own_at = lax.dynamic_index_in_dim(position, data_rank, 0, keepdims=False)
    hit = (own_at[None, :] == jnp.arange(capacity, dtype=jnp.int32)[:, None]) & (
        own_mask[None, :] == 1
    )
    within = jnp.sum(
        jnp.where(hit, jnp.arange(down * across, dtype=jnp.int32)[None, :], 0), axis=1
    )
    packed_in, packed_out = pack(
        within // across, within % across, weight_in, weight_out, capacity
    )
    gathered_in, gathered_out = gather(packed_in, packed_out, peers)

    by_hidden = pair_lists(strip, slot, 0, slots)
    by_row = pair_lists(strip, slot, 1, slots)

    active = run(
        hidden_kernel, "hidden", by_hidden, (tokens, gathered_in), across, jnp.bfloat16
    )
    partial = run(emit_kernel, "emit", by_row, (active, gathered_out), all_rows, jnp.bfloat16)
    whole_out = lax.psum(partial, "tensor")
    goal = run(
        goal_kernel, "goal", by_hidden, (target, gathered_out, active), across, jnp.float32
    )
    share = whole_out.shape[1] // lax.axis_size("tensor")
    output = lax.dynamic_slice_in_dim(whole_out, tensor_rank * share, share, 1)
    result = run(
        correct_kernel, "correct", by_hidden, (whole_out, gathered_out, goal), across, jnp.bfloat16
    )
    return output, result


def solution(mesh):
    in_specs = (P("dp", None), P("dp", None), P("dp", "tensor"), P("tensor", "dp"), P())
    out_specs = (P("dp", "tensor"), P("dp", "tensor"))
    return jax.shard_map(shards, mesh=mesh, in_specs=in_specs, out_specs=out_specs, check_vma=False)
```

```python
import jax
import jax.numpy as jnp
from jax import lax
from jax.experimental import pallas as pl
from jax.experimental.pallas import tpu as pltpu
from jax.sharding import PartitionSpec as P

BLK = 128
UNROLL = 8
PIECES = 4
STRIPS = 4
VMEM_CAP = 60 * 1024 * 1024


def tile_slots(strip, peer_count, capacity):
    rows, across = strip.shape
    flat = strip.reshape(peer_count, rows // peer_count * across)
    position = jnp.cumsum(flat, axis=1) - 1
    base = jnp.arange(peer_count, dtype=jnp.int32)[:, None] * capacity
    return (position + base).reshape(rows, across), position


def pair_lists(strip, slot, axis, slots):
    rows, across = strip.shape
    kept = strip.shape[1 - axis]
    pairs = -(-((slots + kept) // 2) // UNROLL) * UNROLL
    rank = jnp.cumsum(strip, axis=axis) - 1
    runs = (jnp.sum(strip, axis=axis) + 1) // 2
    start = 2 * (jnp.cumsum(runs) - runs)
    place = rank + jnp.expand_dims(start, axis)
    row = lax.broadcasted_iota(jnp.int32, strip.shape, 0)
    column = lax.broadcasted_iota(jnp.int32, strip.shape, 1)
    code = ((slot + 1) * rows + row) * across + column
    place = jnp.where(strip == 1, place, -1).reshape(1, -1)
    hit = place == jnp.arange(2 * pairs, dtype=jnp.int32)[:, None]
    found = jnp.sum(jnp.where(hit, code.reshape(1, -1), 0), axis=1)
    valid = (found > 0).astype(jnp.int32)
    source = jnp.maximum(found // (rows * across) - 1, 0)
    row_of = (found // across) % rows
    column_of = found % across
    over, along = (row_of, column_of) if axis == 0 else (column_of, row_of)
    return source, over, along[::2], valid


def pack_kernel(rows_ref, cols_ref, in_ref, out_ref, packed_in, packed_out, sems):
    count = packed_in.shape[0]

    def start(s, carry):
        r = pl.multiple_of(rows_ref[s] * BLK, BLK)
        j = pl.multiple_of(cols_ref[s] * BLK, BLK)
        pltpu.make_async_copy(
            in_ref.at[pl.ds(r, BLK), pl.ds(j, BLK)], packed_in.at[s], sems.at[0]
        ).start()
        pltpu.make_async_copy(
            out_ref.at[pl.ds(j, BLK), pl.ds(r, BLK)], packed_out.at[s], sems.at[1]
        ).start()
        return carry

    lax.fori_loop(0, count, start, 0)
    pltpu.make_async_copy(packed_in, packed_in, sems.at[0]).wait()
    pltpu.make_async_copy(packed_out, packed_out, sems.at[1]).wait()


def pack(rows, cols, weight_in, weight_out, capacity):
    shape = jax.ShapeDtypeStruct((capacity, BLK, BLK), jnp.bfloat16)
    return pl.pallas_call(
        pack_kernel,
        grid_spec=pltpu.PrefetchScalarGridSpec(
            num_scalar_prefetch=2,
            grid=(1,),
            in_specs=[pl.BlockSpec(memory_space=pl.ANY)] * 2,
            out_specs=[pl.BlockSpec((capacity, BLK, BLK), lambda i, *_: (0, 0, 0))] * 2,
            scratch_shapes=[pltpu.SemaphoreType.DMA((2,))],
        ),
        out_shape=(shape, shape),
        name="pack",
    )(rows, cols, weight_in, weight_out)


def gather_kernel(in_ref, out_ref, all_in, all_out, send, recv, local):
    me = lax.axis_index("dp")
    core, x, y = me % 2, (me // 2) % 2, me // 4

    def index(c, x_at, y_at):
        return (y_at * 2 + x_at) * 2 + c

    beside = index(core, 1 - x, y)
    above = index(core, x, 1 - y)
    across = index(core, 1 - x, 1 - y)
    partner = index(1 - core, x, y)
    barrier = pltpu.get_barrier_semaphore()
    for other in (beside, above, partner):
        pl.semaphore_signal(
            barrier, inc=1, device_id={"dp": other}, device_id_type=pl.DeviceIdType.MESH
        )
    pl.semaphore_wait(barrier, 3)

    count = in_ref.shape[0]
    pieces = PIECES if count % PIECES == 0 else 1
    size = count // pieces
    steps = range(2 * pieces)

    def own(k):
        return (in_ref, out_ref)[k // pieces].at[pl.ds((k % pieces) * size, size)]

    def held(owner, k):
        ref = (all_in, all_out)[k // pieces]
        return ref.at[pl.ds(owner * count + (k % pieces) * size, size)]

    started = []

    def move(path, k, source, owner, to):
        copy = pltpu.make_async_remote_copy(
            src_ref=source,
            dst_ref=held(owner, k),
            send_sem=send.at[path, k],
            recv_sem=recv.at[path, k],
            device_id={"dp": to},
            device_id_type=pl.DeviceIdType.MESH,
        )
        copy.start()
        started.append(copy)

    def arrive(path, k, owner, to):
        pltpu.make_async_remote_copy(
            src_ref=held(owner, k),
            dst_ref=held(owner, k),
            send_sem=send.at[path, k],
            recv_sem=recv.at[path, k],
            device_id={"dp": to},
            device_id_type=pl.DeviceIdType.MESH,
        ).wait_recv()

    for k in steps:
        move(0, k, own(k), me, beside)
        move(1, k, own(k), me, above)
        move(2, k, own(k), me, partner)
    copies = [
        pltpu.make_async_copy(own(k), held(me, k), local.at[k]) for k in steps
    ]
    for copy in copies:
        copy.start()
    for k in steps:
        arrive(0, k, beside, beside)
        if k % 2 == 0:
            move(3, k, held(beside, k), beside, above)
        move(5, k, held(beside, k), beside, partner)
        arrive(1, k, above, above)
        if k % 2 == 1:
            move(4, k, held(above, k), above, beside)
        move(6, k, held(above, k), above, partner)
    for k in steps:
        if k % 2 == 0:
            arrive(3, k, across, above)
        else:
            arrive(4, k, across, beside)
        move(7, k, held(across, k), across, partner)
    for k in steps:
        arrive(2, k, partner, partner)
        arrive(5, k, index(1 - core, 1 - x, y), partner)
        arrive(6, k, index(1 - core, x, 1 - y), partner)
        arrive(7, k, index(1 - core, 1 - x, 1 - y), partner)
    for copy in started:
        copy.wait_send()
    for copy in copies:
        copy.wait()


def gather(packed_in, packed_out, peers):
    if peers != 8:
        return (
            lax.all_gather(packed_in, "dp", axis=0, tiled=True),
            lax.all_gather(packed_out, "dp", axis=0, tiled=True),
        )
    count = packed_in.shape[0]
    shape = jax.ShapeDtypeStruct((peers * count, BLK, BLK), jnp.bfloat16)
    pieces = PIECES if count % PIECES == 0 else 1
    return pl.pallas_call(
        gather_kernel,
        out_shape=(shape, shape),
        in_specs=[pl.BlockSpec(memory_space=pltpu.VMEM)] * 2,
        out_specs=[pl.BlockSpec(memory_space=pl.ANY)] * 2,
        scratch_shapes=[
            pltpu.SemaphoreType.DMA((8, 2 * pieces)),
            pltpu.SemaphoreType.DMA((8, 2 * pieces)),
            pltpu.SemaphoreType.DMA((2 * pieces,)),
        ],
        compiler_params=pltpu.CompilerParams(collective_id=0, has_side_effects=True),
        name="gather",
    )(packed_in, packed_out)


def total_kernel(n, part, total, from_left, from_right, to_right, to_left, send, recv):
    t = lax.axis_index("tensor")
    right, left = (t + 1) % n, (t + n - 1) % n
    barrier = pltpu.get_barrier_semaphore()

    @pl.when(t > 0)
    def _():
        pl.semaphore_signal(
            barrier, inc=1, device_id={"tensor": left}, device_id_type=pl.DeviceIdType.MESH
        )

    @pl.when(t < n - 1)
    def _():
        pl.semaphore_signal(
            barrier, inc=1, device_id={"tensor": right}, device_id_type=pl.DeviceIdType.MESH
        )

    inner = (t > 0) & (t < n - 1)

    @pl.when(inner)
    def _():
        pl.semaphore_wait(barrier, 2)

    @pl.when(jnp.logical_not(inner))
    def _():
        pl.semaphore_wait(barrier, 1)

    rows, width = part.shape
    share = width // n
    size = rows // STRIPS

    def at(ref, s, c):
        if ref is part or ref is total:
            return ref.at[pl.ds(c * size, size), pl.ds(s * share, share)]
        return ref.at[s, pl.ds(c * size, size)]

    def copy(path, s, c, source, landing):
        return pltpu.make_async_remote_copy(
            src_ref=at(source, s, c),
            dst_ref=at(landing, s, c),
            send_sem=send.at[path, s, c],
            recv_sem=recv.at[path, s, c],
            device_id={"tensor": right if path % 2 == 0 else left},
            device_id_type=pl.DeviceIdType.MESH,
        )

    def landed(path, s, c, landing):
        copy(path, s, c, landing, landing).wait_recv()

    def add(s, c, *refs):
        value = at(part, s, c)[...].astype(jnp.float32)
        for ref in refs:
            value = value + at(ref, s, c)[...].astype(jnp.float32)
        return value.astype(part.dtype)

    def inward(c):
        for path, order, landing, stage in (
            (0, range(n - 1, 0, -1), from_left, to_right),
            (1, range(n - 1), from_right, to_left),
        ):
            first = 0 if path == 0 else n - 1
            for s in order:

                @pl.when(t == first)
                def _():
                    copy(path, s, c, part, landing).start()

                @pl.when((t > 0) & (t < s) if path == 0 else (t < n - 1) & (t > s))
                def _():
                    landed(path, s, c, landing)
                    at(stage, s, c)[...] = add(s, c, landing)
                    copy(path, s, c, stage, landing).start()

    def finish(c):
        for s in range(n):

            @pl.when(t == s)
            def _():
                refs = []
                if s > 0:
                    landed(0, s, c, from_left)
                    refs.append(from_left)
                if s < n - 1:
                    landed(1, s, c, from_right)
                    refs.append(from_right)
                at(total, s, c)[...] = add(s, c, *refs)
                if s < n - 1:
                    copy(2, s, c, total, total).start()
                if s > 0:
                    copy(3, s, c, total, total).start()

    def outward(c):
        for distance in range(1, n):
            for s in range(n):
                if s + distance < n:

                    @pl.when(t == s + distance)
                    def _():
                        landed(2, s, c, total)
                        if s + distance < n - 1:
                            copy(2, s, c, total, total).start()

                if s - distance >= 0:

                    @pl.when(t == s - distance)
                    def _():
                        landed(3, s, c, total)
                        if s - distance > 0:
                            copy(3, s, c, total, total).start()

    for c in range(STRIPS + 2):
        if c < STRIPS:
            inward(c)
        if 1 <= c < STRIPS + 1:
            finish(c - 1)
        if c >= 2:
            outward(c - 2)

    for c in range(STRIPS):
        for s in range(n):
            for path in range(4):
                landing = (from_left, from_right, total, total)[path]
                sent = (t < s, t > s, (t >= s) & (t < n - 1), (t <= s) & (t > 0))[path]

                @pl.when(sent)
                def _():
                    copy(path, s, c, landing, landing).wait_send()


def total_of(partial, n):
    rows, width = partial.shape
    if n == 1:
        return partial
    buffer = pltpu.VMEM((n, rows, width // n), partial.dtype)
    return pl.pallas_call(
        lambda *refs: total_kernel(n, *refs),
        out_shape=jax.ShapeDtypeStruct(partial.shape, partial.dtype),
        in_specs=[pl.BlockSpec(memory_space=pltpu.VMEM)],
        out_specs=pl.BlockSpec(memory_space=pltpu.VMEM),
        scratch_shapes=[
            buffer,
            buffer,
            buffer,
            buffer,
            pltpu.SemaphoreType.DMA((4, n, STRIPS)),
            pltpu.SemaphoreType.DMA((4, n, STRIPS)),
        ],
        compiler_params=pltpu.CompilerParams(collective_id=1, has_side_effects=True),
        name="total",
    )(partial)


def sweep(lists, lhs_ref, w_ref, acc, pairs, transposed):
    source, over, along, valid = lists
    acc[...] = jnp.zeros_like(acc)

    def one(p):
        parts, weights = [], []
        for k in (2 * p, 2 * p + 1):
            off = pl.multiple_of(over[k] * BLK, BLK)
            part = lhs_ref[:, pl.ds(off, BLK)]
            parts.append(jnp.where(valid[k] == 1, part, jnp.zeros_like(part)))
            weights.append(w_ref[source[k]])
        lhs = jnp.concatenate(parts, axis=1)
        if transposed:
            rhs = jnp.concatenate(weights, axis=1)
            dims = (((1,), (1,)), ((), ()))
        else:
            rhs = jnp.concatenate(weights, axis=0)
            dims = (((1,), (0,)), ((), ()))
        return along[p], lax.dot_general(lhs, rhs, dims, preferred_element_type=jnp.float32)

    def body(i, carry):
        results = [one(i * UNROLL + u) for u in range(UNROLL)]
        for place, value in results:
            acc[place] += value
        return carry

    lax.fori_loop(0, pairs // UNROLL, body, 0)


def spread(acc, out_ref, finish):
    def body(j, carry):
        at = pl.ds(pl.multiple_of(j * BLK, BLK), BLK)
        out_ref[:, at] = finish(acc[j], at)
        return carry

    lax.fori_loop(0, acc.shape[0], body, 0)


def hidden_kernel(source, over, along, valid, lhs, w, active, acc):
    sweep((source, over, along, valid), lhs, w, acc, along.shape[0], False)
    spread(acc, active, lambda a, at: jnp.tanh(a).astype(jnp.bfloat16))


def emit_kernel(source, over, along, valid, lhs, w, partial, acc):
    sweep((source, over, along, valid), lhs, w, acc, along.shape[0], False)
    spread(acc, partial, lambda a, at: a.astype(jnp.bfloat16))


def goal_kernel(source, over, along, valid, lhs, w, active, goal, acc):
    sweep((source, over, along, valid), lhs, w, acc, along.shape[0], True)
    spread(acc, goal, lambda a, at: active[:, at].astype(jnp.float32) + jnp.tanh(a))


def correct_kernel(source, over, along, valid, lhs, w, goal, result, acc):
    sweep((source, over, along, valid), lhs, w, acc, along.shape[0], True)
    spread(acc, result, lambda a, at: (goal[:, at] - jnp.tanh(a)).astype(jnp.bfloat16))


def run(kernel, name, lists, arrays, blocks, dtype):
    tok = arrays[0].shape[0]
    pairs = lists[2].shape[0]
    return pl.pallas_call(
        kernel,
        grid_spec=pltpu.PrefetchScalarGridSpec(
            num_scalar_prefetch=4,
            grid=(1,),
            in_specs=[
                pl.BlockSpec(a.shape, lambda i, *_, n=a.ndim: (0,) * n, pipeline_mode=pl.Buffered(1))
                for a in arrays
            ],
            out_specs=pl.BlockSpec((tok, blocks * BLK), lambda i, *_: (0, 0)),
            scratch_shapes=[pltpu.VMEM((blocks, tok, BLK), jnp.float32)],
        ),
        out_shape=jax.ShapeDtypeStruct((tok, blocks * BLK), dtype),
        compiler_params=pltpu.CompilerParams(vmem_limit_bytes=VMEM_CAP),
        cost_estimate=pl.CostEstimate(
            flops=pairs * 4 * tok * BLK * BLK * 4,
            bytes_accessed=sum(a.size * a.dtype.itemsize for a in arrays),
            transcendentals=0,
        ),
        name=name,
    )(*lists, *arrays)


def shards(tokens, target, weight_in, weight_out, pattern):
    peers = lax.axis_size("dp")
    data_rank = lax.axis_index("dp")
    tensor_rank = lax.axis_index("tensor")
    down = weight_in.shape[0] // BLK
    across = weight_in.shape[1] // BLK
    capacity = max(2, down * across // 4)
    slots = peers * capacity
    all_rows = tokens.shape[1] // BLK
    strip = lax.dynamic_slice_in_dim(pattern, tensor_rank * across, across, 1)
    slot, position = tile_slots(strip, peers, capacity)

    own_mask = lax.dynamic_index_in_dim(
        strip.reshape(peers, down * across), data_rank, 0, keepdims=False
    )
    own_at = lax.dynamic_index_in_dim(position, data_rank, 0, keepdims=False)
    hit = (own_at[None, :] == jnp.arange(capacity, dtype=jnp.int32)[:, None]) & (
        own_mask[None, :] == 1
    )
    within = jnp.sum(
        jnp.where(hit, jnp.arange(down * across, dtype=jnp.int32)[None, :], 0), axis=1
    )
    packed_in, packed_out = pack(
        within // across, within % across, weight_in, weight_out, capacity
    )
    gathered_in, gathered_out = gather(packed_in, packed_out, peers)

    by_hidden = pair_lists(strip, slot, 0, slots)
    by_row = pair_lists(strip, slot, 1, slots)

    active = run(
        hidden_kernel, "hidden", by_hidden, (tokens, gathered_in), across, jnp.bfloat16
    )
    partial = run(emit_kernel, "emit", by_row, (active, gathered_out), all_rows, jnp.bfloat16)
    whole_out = total_of(partial, lax.axis_size("tensor"))
    goal = run(
        goal_kernel, "goal", by_hidden, (target, gathered_out, active), across, jnp.float32
    )
    share = whole_out.shape[1] // lax.axis_size("tensor")
    output = lax.dynamic_slice_in_dim(whole_out, tensor_rank * share, share, 1)
    result = run(
        correct_kernel, "correct", by_hidden, (whole_out, gathered_out, goal), across, jnp.bfloat16
    )
    return output, result


def solution(mesh):
    in_specs = (P("dp", None), P("dp", None), P("dp", "tensor"), P("tensor", "dp"), P())
    out_specs = (P("dp", "tensor"), P("dp", "tensor"))
    return jax.shard_map(shards, mesh=mesh, in_specs=in_specs, out_specs=out_specs, check_vma=False)
```

```python
import jax
import jax.numpy as jnp
from jax import lax
from jax.experimental import pallas as pl
from jax.experimental.pallas import tpu as pltpu
from jax.sharding import PartitionSpec as P

BLK = 128
UNROLL = 16
PIECES = 8
VMEM_CAP = 60 * 1024 * 1024


def tile_slots(strip, peer_count, capacity):
    rows, across = strip.shape
    flat = strip.reshape(peer_count, rows // peer_count * across)
    position = jnp.cumsum(flat, axis=1) - 1
    base = jnp.arange(peer_count, dtype=jnp.int32)[:, None] * capacity
    return (position + base).reshape(rows, across), position


def pair_lists(strip, slot, axis, slots):
    rows, across = strip.shape
    kept = strip.shape[1 - axis]
    pairs = -(-((slots + kept) // 2) // UNROLL) * UNROLL
    rank = jnp.cumsum(strip, axis=axis) - 1
    runs = (jnp.sum(strip, axis=axis) + 1) // 2
    start = 2 * (jnp.cumsum(runs) - runs)
    place = rank + jnp.expand_dims(start, axis)
    row = lax.broadcasted_iota(jnp.int32, strip.shape, 0)
    column = lax.broadcasted_iota(jnp.int32, strip.shape, 1)
    code = ((slot + 1) * rows + row) * across + column
    place = jnp.where(strip == 1, place, -1).reshape(1, -1)
    hit = place == jnp.arange(2 * pairs, dtype=jnp.int32)[:, None]
    found = jnp.sum(jnp.where(hit, code.reshape(1, -1), 0), axis=1)
    valid = (found > 0).astype(jnp.int32)
    source = jnp.maximum(found // (rows * across) - 1, 0)
    row_of = (found // across) % rows
    column_of = found % across
    over, along = (row_of, column_of) if axis == 0 else (column_of, row_of)
    return source, over, along[::2], valid


def pack_kernel(rows_ref, cols_ref, in_ref, out_ref, packed_in, packed_out, sems):
    count = packed_in.shape[0]

    def start(s, carry):
        r = pl.multiple_of(rows_ref[s] * BLK, BLK)
        j = pl.multiple_of(cols_ref[s] * BLK, BLK)
        pltpu.make_async_copy(
            in_ref.at[pl.ds(r, BLK), pl.ds(j, BLK)], packed_in.at[s], sems.at[0]
        ).start()
        pltpu.make_async_copy(
            out_ref.at[pl.ds(j, BLK), pl.ds(r, BLK)], packed_out.at[s], sems.at[1]
        ).start()
        return carry

    lax.fori_loop(0, count, start, 0)
    pltpu.make_async_copy(packed_in, packed_in, sems.at[0]).wait()
    pltpu.make_async_copy(packed_out, packed_out, sems.at[1]).wait()


def pack(rows, cols, weight_in, weight_out, capacity):
    shape = jax.ShapeDtypeStruct((capacity, BLK, BLK), jnp.bfloat16)
    return pl.pallas_call(
        pack_kernel,
        grid_spec=pltpu.PrefetchScalarGridSpec(
            num_scalar_prefetch=2,
            grid=(1,),
            in_specs=[pl.BlockSpec(memory_space=pl.ANY)] * 2,
            out_specs=[pl.BlockSpec((capacity, BLK, BLK), lambda i, *_: (0, 0, 0))] * 2,
            scratch_shapes=[pltpu.SemaphoreType.DMA((2,))],
        ),
        out_shape=(shape, shape),
        name="pack",
    )(rows, cols, weight_in, weight_out)


def gather_kernel(in_ref, out_ref, all_in, all_out, send, recv, local):
    me = lax.axis_index("dp")
    core, x, y = me % 2, (me // 2) % 2, me // 4

    def index(c, x_at, y_at):
        return (y_at * 2 + x_at) * 2 + c

    beside = index(core, 1 - x, y)
    above = index(core, x, 1 - y)
    across = index(core, 1 - x, 1 - y)
    partner = index(1 - core, x, y)
    barrier = pltpu.get_barrier_semaphore()
    for other in (beside, above, partner):
        pl.semaphore_signal(
            barrier, inc=1, device_id={"dp": other}, device_id_type=pl.DeviceIdType.MESH
        )
    pl.semaphore_wait(barrier, 3)

    count = in_ref.shape[0]
    pieces = PIECES if count % PIECES == 0 else 1
    size = count // pieces
    steps = range(2 * pieces)

    def own(k):
        return (in_ref, out_ref)[k // pieces].at[pl.ds((k % pieces) * size, size)]

    def held(owner, k):
        ref = (all_in, all_out)[k // pieces]
        return ref.at[pl.ds(owner * count + (k % pieces) * size, size)]

    started = []

    def move(path, k, source, owner, to):
        copy = pltpu.make_async_remote_copy(
            src_ref=source,
            dst_ref=held(owner, k),
            send_sem=send.at[path, k],
            recv_sem=recv.at[path, k],
            device_id={"dp": to},
            device_id_type=pl.DeviceIdType.MESH,
        )
        copy.start()
        started.append(copy)

    def arrive(path, k, owner, to):
        pltpu.make_async_remote_copy(
            src_ref=held(owner, k),
            dst_ref=held(owner, k),
            send_sem=send.at[path, k],
            recv_sem=recv.at[path, k],
            device_id={"dp": to},
            device_id_type=pl.DeviceIdType.MESH,
        ).wait_recv()

    for k in steps:
        move(0, k, own(k), me, beside)
        move(1, k, own(k), me, above)
        move(2, k, own(k), me, partner)
    copies = [
        pltpu.make_async_copy(own(k), held(me, k), local.at[k]) for k in steps
    ]
    for copy in copies:
        copy.start()
    for k in steps:
        arrive(0, k, beside, beside)
        if k % 2 == 0:
            move(3, k, held(beside, k), beside, above)
        move(5, k, held(beside, k), beside, partner)
        arrive(1, k, above, above)
        if k % 2 == 1:
            move(4, k, held(above, k), above, beside)
        move(6, k, held(above, k), above, partner)
    for k in steps:
        if k % 2 == 0:
            arrive(3, k, across, above)
        else:
            arrive(4, k, across, beside)
        move(7, k, held(across, k), across, partner)
    for k in steps:
        arrive(2, k, partner, partner)
        arrive(5, k, index(1 - core, 1 - x, y), partner)
        arrive(6, k, index(1 - core, x, 1 - y), partner)
        arrive(7, k, index(1 - core, 1 - x, 1 - y), partner)
    for copy in started:
        copy.wait_send()
    for copy in copies:
        copy.wait()


def gather(packed_in, packed_out, peers):
    if peers != 8:
        return (
            lax.all_gather(packed_in, "dp", axis=0, tiled=True),
            lax.all_gather(packed_out, "dp", axis=0, tiled=True),
        )
    count = packed_in.shape[0]
    shape = jax.ShapeDtypeStruct((peers * count, BLK, BLK), jnp.bfloat16)
    pieces = PIECES if count % PIECES == 0 else 1
    return pl.pallas_call(
        gather_kernel,
        out_shape=(shape, shape),
        in_specs=[pl.BlockSpec(memory_space=pltpu.VMEM)] * 2,
        out_specs=[pl.BlockSpec(memory_space=pl.ANY)] * 2,
        scratch_shapes=[
            pltpu.SemaphoreType.DMA((8, 2 * pieces)),
            pltpu.SemaphoreType.DMA((8, 2 * pieces)),
            pltpu.SemaphoreType.DMA((2 * pieces,)),
        ],
        compiler_params=pltpu.CompilerParams(collective_id=0, has_side_effects=True),
        name="gather",
    )(packed_in, packed_out)


def sweep(lists, lhs_ref, w_ref, acc, pairs, transposed):
    source, over, along, valid = lists
    acc[...] = jnp.zeros_like(acc)

    def one(p):
        parts, weights = [], []
        for k in (2 * p, 2 * p + 1):
            off = pl.multiple_of(over[k] * BLK, BLK)
            part = lhs_ref[:, pl.ds(off, BLK)]
            parts.append(jnp.where(valid[k] == 1, part, jnp.zeros_like(part)))
            weights.append(w_ref[source[k]])
        lhs = jnp.concatenate(parts, axis=1)
        if transposed:
            rhs = jnp.concatenate(weights, axis=1)
            dims = (((1,), (1,)), ((), ()))
        else:
            rhs = jnp.concatenate(weights, axis=0)
            dims = (((1,), (0,)), ((), ()))
        return along[p], lax.dot_general(lhs, rhs, dims, preferred_element_type=jnp.float32)

    def body(i, carry):
        results = [one(i * UNROLL + u) for u in range(UNROLL)]
        for place, value in results:
            acc[place] += value
        return carry

    lax.fori_loop(0, pairs // UNROLL, body, 0)


def spread(acc, out_ref, finish):
    def body(j, carry):
        at = pl.ds(pl.multiple_of(j * BLK, BLK), BLK)
        out_ref[:, at] = finish(acc[j], at)
        return carry

    lax.fori_loop(0, acc.shape[0], body, 0)


def hidden_kernel(source, over, along, valid, lhs, w, active, acc):
    sweep((source, over, along, valid), lhs, w, acc, along.shape[0], False)
    spread(acc, active, lambda a, at: jnp.tanh(a).astype(jnp.bfloat16))


def emit_kernel(source, over, along, valid, lhs, w, partial, acc):
    sweep((source, over, along, valid), lhs, w, acc, along.shape[0], False)
    spread(acc, partial, lambda a, at: a.astype(jnp.bfloat16))


def goal_kernel(source, over, along, valid, lhs, w, active, goal, acc):
    sweep((source, over, along, valid), lhs, w, acc, along.shape[0], True)
    spread(acc, goal, lambda a, at: active[:, at].astype(jnp.float32) + jnp.tanh(a))


def correct_kernel(source, over, along, valid, lhs, w, goal, result, acc):
    sweep((source, over, along, valid), lhs, w, acc, along.shape[0], True)
    spread(acc, result, lambda a, at: (goal[:, at] - jnp.tanh(a)).astype(jnp.bfloat16))


def run(kernel, name, lists, arrays, blocks, dtype):
    tok = arrays[0].shape[0]
    pairs = lists[2].shape[0]
    return pl.pallas_call(
        kernel,
        grid_spec=pltpu.PrefetchScalarGridSpec(
            num_scalar_prefetch=4,
            grid=(1,),
            in_specs=[
                pl.BlockSpec(a.shape, lambda i, *_, n=a.ndim: (0,) * n, pipeline_mode=pl.Buffered(1))
                for a in arrays
            ],
            out_specs=pl.BlockSpec((tok, blocks * BLK), lambda i, *_: (0, 0)),
            scratch_shapes=[pltpu.VMEM((blocks, tok, BLK), jnp.float32)],
        ),
        out_shape=jax.ShapeDtypeStruct((tok, blocks * BLK), dtype),
        compiler_params=pltpu.CompilerParams(vmem_limit_bytes=VMEM_CAP),
        cost_estimate=pl.CostEstimate(
            flops=pairs * 4 * tok * BLK * BLK * 4,
            bytes_accessed=sum(a.size * a.dtype.itemsize for a in arrays),
            transcendentals=0,
        ),
        name=name,
    )(*lists, *arrays)


def shards(tokens, target, weight_in, weight_out, pattern):
    peers = lax.axis_size("dp")
    data_rank = lax.axis_index("dp")
    tensor_rank = lax.axis_index("tensor")
    down = weight_in.shape[0] // BLK
    across = weight_in.shape[1] // BLK
    capacity = max(2, down * across // 4)
    slots = peers * capacity
    all_rows = tokens.shape[1] // BLK
    strip = lax.dynamic_slice_in_dim(pattern, tensor_rank * across, across, 1)
    slot, position = tile_slots(strip, peers, capacity)

    own_mask = lax.dynamic_index_in_dim(
        strip.reshape(peers, down * across), data_rank, 0, keepdims=False
    )
    own_at = lax.dynamic_index_in_dim(position, data_rank, 0, keepdims=False)
    hit = (own_at[None, :] == jnp.arange(capacity, dtype=jnp.int32)[:, None]) & (
        own_mask[None, :] == 1
    )
    within = jnp.sum(
        jnp.where(hit, jnp.arange(down * across, dtype=jnp.int32)[None, :], 0), axis=1
    )
    packed_in, packed_out = pack(
        within // across, within % across, weight_in, weight_out, capacity
    )
    gathered_in, gathered_out = gather(packed_in, packed_out, peers)

    by_hidden = pair_lists(strip, slot, 0, slots)
    by_row = pair_lists(strip, slot, 1, slots)

    active = run(
        hidden_kernel, "hidden", by_hidden, (tokens, gathered_in), across, jnp.bfloat16
    )
    partial = run(emit_kernel, "emit", by_row, (active, gathered_out), all_rows, jnp.bfloat16)
    whole_out = lax.psum(partial, "tensor")
    goal = run(
        goal_kernel, "goal", by_hidden, (target, gathered_out, active), across, jnp.float32
    )
    share = whole_out.shape[1] // lax.axis_size("tensor")
    output = lax.dynamic_slice_in_dim(whole_out, tensor_rank * share, share, 1)
    result = run(
        correct_kernel, "correct", by_hidden, (whole_out, gathered_out, goal), across, jnp.bfloat16
    )
    return output, result


def solution(mesh):
    in_specs = (P("dp", None), P("dp", None), P("dp", "tensor"), P("tensor", "dp"), P())
    out_specs = (P("dp", "tensor"), P("dp", "tensor"))
    return jax.shard_map(shards, mesh=mesh, in_specs=in_specs, out_specs=out_specs, check_vma=False)
```
